128 devices in a mesh: dp: 16 (over z, x), head: 8 (over y, core).
Axes of the slice: x: 4, y: 4, z: 4, core: 2. Of those that a mesh axis runs over, the one named last changes fastest.
Arguments:
- prefill_query: bfloat16 [16384, 8192], P(('dp', 'head')), may hold values from -20 to 20
- prefill_pairs: bfloat16 [16384, 2048], P(('dp', 'head')), may hold values from -4 to 4
- decode_query: bfloat16 [128, 8192], P(('dp', 'head')), may hold values from -20 to 20
- decode_pairs: bfloat16 [128, 2048], P(('dp', 'head')), may hold values from -4 to 4
- cache_pool: bfloat16 [2560, 8, 64, 256], P('dp', 'head'), may hold values from -11 to 11
- decode_pages: int32 [128, 16], P('dp'), may hold values from 0 to 159, as said below
- prefill_pages: int32 [16, 32], P('dp'), may hold values from 0 to 159, as said below
- cache_length: int32 [128], replicated, may hold values from 1 to 1023, as said below
- prefix_length: int32 [16], P('dp'), may hold values from 0 to 1024, as said below
- migrant_slot: int32 [16, 1], replicated, may hold values from 0 to 7, as said below
- migrant_target: int32 [16, 1], replicated, may hold values from 0 to 15, as said below
- arrivals: int32 [128], replicated, may hold values from 0 to 127, each once
Outputs:
- prefill_attended: bfloat16 [16384, 8192], P(('dp', 'head'))
- decode_attended: bfloat16 [128, 8192], P('dp', 'head')
- updated_pool: bfloat16 [2560, 8, 64, 256], P('dp', 'head')
The draws below stay inside these ranges and needn't reach their ends.
Inputs may be any that keep to these rules, and one draw needn't show every extreme that they name: Page numbers within the group's pool; in each group the entries of its 8 rows of decode_pages and its row of prefill_pages are all different. `prefill_pages`: see decode_pages. `cache_length`: A migrating request holds at most 255 cached tokens, and one holds exactly 255. `prefix_length`: A multiple of 64. `migrant_slot`: the slots of one group are all different. `migrant_target`: each column is a permutation of the groups: every group receives exactly one request of each column; a request may stay in its group.
All inputs are finite; a program needn't handle non-finite values.
Results may differ from the reference program's by a relative error of at most 0.008.
Values may be sent and summed in bfloat16 or wider, within the bound.
A program may use at most 128 MiB of HBM per device.

```python
import jax
import jax.numpy as jnp
from jax import lax

QH = 64
KVH = 8
HD = 128
QPK = 8
PAGE = 64
L = 1024
MAXP = 16
RD_DEV = 8
CH = 1024
PMAX = 1024
PREP = 32
MIG_DEV = 1
MIGP = 4
MIGL = 255
POOL_DEV = 160
RD = 128
N_DP = 16


def slot_plan(key):

    def one_order(subkey):
        return jax.random.permutation(subkey, RD_DEV)
    slot_order = jax.vmap(one_order)(jax.random.split(jax.random.fold_in(key, 201), N_DP)).astype(jnp.int32)
    chosen = jax.random.randint(jax.random.fold_in(key, 202), (), 0, N_DP)
    second = (chosen + 1) % N_DP
    shifts = jnp.zeros((N_DP,), jnp.int32)
    shifts = shifts.at[chosen].set((RD_DEV - 1 - slot_order[chosen, 0]) % RD_DEV)
    shifts = shifts.at[second].set((0 - slot_order[second, 0]) % RD_DEV)
    slot_order = (slot_order + shifts[:, None]) % RD_DEV
    lengths = jax.random.randint(jax.random.fold_in(key, 203), (N_DP, RD_DEV), 1, L)
    short_len = jax.random.randint(jax.random.fold_in(key, 204), (N_DP, MIG_DEV), 1, MIGL + 1)
    group_rows = jnp.arange(N_DP, dtype=jnp.int32)[:, None]
    lengths = lengths.at[group_rows, slot_order[:, :MIG_DEV]].set(short_len)
    lengths = lengths.at[chosen, slot_order[chosen, MIG_DEV]].set(L - 1)
    lengths = lengths.at[second, slot_order[second, MIG_DEV]].set(1)
    lengths = lengths.at[second, slot_order[second, 0]].set(MIGL)
    return (slot_order, lengths.astype(jnp.int32))


def page_plan(key):

    def one_pool(subkey):
        return jax.random.permutation(subkey, POOL_DEV)
    perms = jax.vmap(one_pool)(jax.random.split(jax.random.fold_in(key, 301), N_DP)).astype(jnp.int32)
    first_group = jax.random.randint(jax.random.fold_in(key, 302), (), 0, N_DP)
    split_at = RD_DEV * MAXP
    shifts = jnp.zeros((N_DP,), jnp.int32)
    for group_step, position, page_value in [(0, 0, POOL_DEV - 1), (1, 0, 0), (2, split_at, POOL_DEV - 1), (3, split_at, 0)]:
        which = (first_group + group_step) % N_DP
        shifts = shifts.at[which].set((page_value - perms[which, position]) % POOL_DEV)
    perms = (perms + shifts[:, None]) % POOL_DEV
    return (perms[:, :split_at].reshape(RD, MAXP), perms[:, split_at:])


def decode_pair_base(key):
    return jnp.clip(jax.random.normal(jax.random.fold_in(key, 501), (RD, KVH, 2 * HD), jnp.float32), -4.0, 4.0)


def draw_decode_pages(key, part):
    return page_plan(key)[0].astype(jnp.int32)


def draw_prefill_pages(key, part):
    return page_plan(key)[1].astype(jnp.int32)


def draw_cache_length(key, part):
    return slot_plan(key)[1].reshape(RD)


def draw_migrant_slot(key, part):
    return slot_plan(key)[0][:, :MIG_DEV].astype(jnp.int32)


def draw_migrant_target(key, part):

    def one_perm(subkey):
        return jax.random.permutation(subkey, N_DP)
    perms = jax.vmap(one_perm)(jax.random.split(jax.random.fold_in(key, 401), MIG_DEV))
    return perms.T.astype(jnp.int32)


def draw_prefix_length(key, part):
    base = PAGE * jax.random.randint(jax.random.fold_in(key, 451), (N_DP,), 0, PMAX // PAGE + 1)
    chosen = jax.random.randint(jax.random.fold_in(key, 452), (), 0, N_DP)
    base = base.at[chosen].set(PMAX).at[(chosen + 1) % N_DP].set(0)
    return base.astype(jnp.int32)


def draw_decode_pairs(key, part):
    return decode_pair_base(key).reshape(RD, KVH * 2 * HD).astype(jnp.bfloat16)


def draw_decode_query(key, part):
    pairs = decode_pair_base(key)
    noise = jnp.clip(jax.random.normal(jax.random.fold_in(key, 601), (RD, KVH, QPK, HD), jnp.float32), -4.0, 4.0)
    values = noise + 0.4 * pairs[:, :, None, :HD]
    return values.reshape(RD, QH * HD).astype(jnp.bfloat16)


def draw_prefill_query(key, part):
    rows = N_DP * CH
    noise = jnp.clip(jax.random.normal(jax.random.fold_in(key, 701), (rows, QH, HD), jnp.float32), -4.0, 4.0)
    values = noise
    return values.reshape(rows, QH * HD).astype(jnp.bfloat16)


def draw_cache_pool(key, part):
    shape = (N_DP * POOL_DEV, KVH, PAGE, 2 * HD)
    values = jnp.clip(jax.random.normal(jax.random.fold_in(key, 801), shape, jnp.float32), -4.0, 4.0)
    return values.astype(jnp.bfloat16)


def shard_levels(key, shape, shards, low, top_value):
    def one(axis_at, parts):
        heights = jax.random.uniform(jax.random.fold_in(jax.random.fold_in(key, 6), axis_at), (parts,), jnp.float32, low / len(shards), top_value / len(shards))
        return jnp.repeat(jnp.exp(heights), shape[axis_at] // parts).reshape((-1,) + (1,) * (len(shape) - axis_at - 1))

    gain = one(*shards[0])
    for cut in shards[1:]:
        gain = gain * one(*cut)
    return gain


def bell_draw(stream_key, shape, width, reach, shards=(), kind=jnp.bfloat16):
    entries = width * jax.random.normal(stream_key, shape, jnp.float32)
    if shards:
        entries = entries * shard_levels(stream_key, shape, shards, -0.22, 0.18)
    return jnp.clip(entries, -reach, reach).astype(kind)


def setup_inputs(seed: int = 0) -> dict:
    key_list = jax.random.split(jax.random.key(seed), 13)
    return {
        "prefill_query": draw_prefill_query(jax.random.fold_in(key_list[12], 71), 0),
        "prefill_pairs": bell_draw(key_list[1], (N_DP * CH, KVH * 2 * HD), 1.0, 4.0, ((0, 128),)),
        "decode_query": draw_decode_query(jax.random.fold_in(key_list[12], 71), 0),
        "decode_pairs": draw_decode_pairs(jax.random.fold_in(key_list[12], 71), 0),
        "cache_pool": draw_cache_pool(jax.random.fold_in(key_list[12], 71), 0),
        "decode_pages": draw_decode_pages(jax.random.fold_in(key_list[12], 71), 0),
        "prefill_pages": draw_prefill_pages(jax.random.fold_in(key_list[12], 71), 0),
        "cache_length": draw_cache_length(jax.random.fold_in(key_list[12], 71), 0),
        "prefix_length": draw_prefix_length(jax.random.fold_in(key_list[12], 71), 0),
        "migrant_slot": draw_migrant_slot(jax.random.fold_in(key_list[12], 71), 0),
        "migrant_target": draw_migrant_target(jax.random.fold_in(key_list[12], 71), 0),
        "arrivals": jax.random.permutation(key_list[11], RD).astype(jnp.int32),
    }


big_negative = -1e30


def reference(prefill_query, prefill_pairs, decode_query, decode_pairs, cache_pool, decode_pages, prefill_pages, cache_length, prefix_length, migrant_slot, migrant_target, arrivals):
    inv_scale = HD ** -0.5
    group_ids = jnp.arange(N_DP, dtype=jnp.int32)
    column_ids = jnp.arange(MIG_DEV, dtype=jnp.int32)
    source_slot = group_ids[:, None] * RD_DEV + migrant_slot
    target_slot = migrant_target * RD_DEV + migrant_slot[migrant_target, column_ids[None, :]]
    source_pages = group_ids[:, None, None] * POOL_DEV + decode_pages[source_slot][:, :, :MIGP]
    target_pages = migrant_target[:, :, None] * POOL_DEV + decode_pages[target_slot][:, :, :MIGP]
    moved_pool = cache_pool.at[target_pages.reshape(-1)].set(cache_pool[source_pages.reshape(-1)])
    lengths = cache_length.at[target_slot.reshape(-1)].set(cache_length[source_slot.reshape(-1)])
    slot_query = jnp.zeros_like(decode_query).at[arrivals].set(decode_query)
    slot_pairs = jnp.zeros_like(decode_pairs).at[arrivals].set(decode_pairs)
    slot_group = jnp.arange(RD, dtype=jnp.int32) // RD_DEV
    page_index = (lengths // PAGE).astype(jnp.int32)
    page_now = slot_group * POOL_DEV + jnp.take_along_axis(decode_pages, page_index[:, None], axis=1)[:, 0]
    appended_pool = moved_pool.at[page_now, :, lengths % PAGE, :].set(slot_pairs.reshape(RD, KVH, 2 * HD))
    first_page = (prefix_length // PAGE).astype(jnp.int32)
    span_index = first_page[:, None] + jnp.arange(CH // PAGE, dtype=jnp.int32)[None, :]
    span_pages = group_ids[:, None] * POOL_DEV + jnp.take_along_axis(prefill_pages, span_index, axis=1)
    span_pairs = prefill_pairs.reshape(N_DP, CH // PAGE, PAGE, KVH, 2 * HD).transpose(0, 1, 3, 2, 4)
    updated_pool = appended_pool.at[span_pages.reshape(-1)].set(span_pairs.reshape(-1, KVH, PAGE, 2 * HD))

    def decode_group(block_items):
        queries, table, slot_len, base = block_items
        key_pages = updated_pool[base + table]
        grouped = queries.reshape(RD_DEV, KVH, QPK, HD).astype(jnp.float32)
        scores = jnp.einsum("skqd,smkpd->skqmp", grouped, key_pages[..., :HD].astype(jnp.float32)) * inv_scale
        position = jnp.arange(MAXP, dtype=jnp.int32)[:, None] * PAGE + jnp.arange(PAGE, dtype=jnp.int32)[None, :]
        visible = position[None, None, None] <= slot_len[:, None, None, None, None]
        masked = jnp.where(visible, scores, big_negative)
        row_top = jnp.max(masked, axis=(3, 4), keepdims=True)
        weights = jnp.where(visible, jnp.exp(masked - row_top), 0.0)
        weight_sum = jnp.sum(weights, axis=(3, 4))
        rounded = lax.optimization_barrier(weights.astype(jnp.bfloat16)).astype(jnp.float32)
        mixed_sum = jnp.einsum("skqmp,smkpd->skqd", rounded, key_pages[..., HD:].astype(jnp.float32))
        return (mixed_sum / weight_sum[..., None]).reshape(RD_DEV, QH * HD).astype(jnp.bfloat16)

    decode_attended = lax.map(decode_group, (slot_query.reshape(N_DP, RD_DEV, QH * HD), decode_pages.reshape(N_DP, RD_DEV, MAXP), lengths.reshape(N_DP, RD_DEV), group_ids * POOL_DEV)).reshape(RD, QH * HD)

    def prefill_group(block_items):
        queries, table, prefix, base = block_items
        key_pages = updated_pool[base + table]
        position = jnp.arange(PREP, dtype=jnp.int32)[:, None] * PAGE + jnp.arange(PAGE, dtype=jnp.int32)[None, :]
        limit = prefix + jnp.arange(CH, dtype=jnp.int32)
        visible = position[None] <= limit[:, None, None]
        grouped = queries.reshape(CH, KVH, QPK, HD).transpose(1, 0, 2, 3)

        def one_head(head_items):
            head_query, head_pages = head_items
            scores = jnp.einsum("tqd,mpd->qtmp", head_query.astype(jnp.float32), head_pages[..., :HD].astype(jnp.float32)) * inv_scale
            masked = jnp.where(visible[None], scores, big_negative)
            row_top = jnp.max(masked, axis=(2, 3), keepdims=True)
            weights = jnp.where(visible[None], jnp.exp(masked - row_top), 0.0)
            weight_sum = jnp.sum(weights, axis=(2, 3))
            rounded = lax.optimization_barrier(weights.astype(jnp.bfloat16)).astype(jnp.float32)
            mixed_sum = jnp.einsum("qtmp,mpd->tqd", rounded, head_pages[..., HD:].astype(jnp.float32))
            return (mixed_sum / weight_sum.T[..., None]).astype(jnp.bfloat16)

        head_out = lax.map(one_head, (grouped, key_pages.transpose(1, 0, 2, 3)))
        return head_out.transpose(1, 0, 2, 3).reshape(CH, QH * HD)

    prefill_attended = lax.map(prefill_group, (prefill_query.reshape(N_DP, CH, QH * HD), prefill_pages, prefix_length, group_ids * POOL_DEV)).reshape(N_DP * CH, QH * HD)
    return prefill_attended, decode_attended, updated_pool
```

```python
import jax
import jax.numpy as jnp
from jax import lax
from jax.experimental import pallas as pl
from jax.experimental.pallas import tpu as pltpu
from jax.sharding import PartitionSpec as P

HD = 128
PAGE = 64
MIGP = 4
QPK = 8
NX = 4
LOG2E = 1.4426950408889634
NEG = -1e30
NT = (((1,), (1,)), ((), ()))


def attend_tile(q, k, v, row0, mask_rows):
    keys = k.shape[0]
    scores = lax.dot_general(q, k, NT, preferred_element_type=jnp.float32)
    tail = scores[:, keys - 256 :]
    row = lax.broadcasted_iota(jnp.int32, tail.shape, 0) % mask_rows + row0
    col = lax.broadcasted_iota(jnp.int32, tail.shape, 1)
    tail = jnp.where(col <= row, tail, NEG)
    scores = jnp.concatenate([scores[:, : keys - 256], tail], axis=1)
    top = jnp.max(scores, axis=1, keepdims=True)
    weights = jnp.exp2((scores - top) * (HD**-0.5 * LOG2E)).astype(jnp.bfloat16)
    mixed = jnp.dot(weights, v, preferred_element_type=jnp.float32)
    return mixed[:, :HD] / mixed[:, HD : HD + 1]


def prefill_kernel(table, prefix, q_ref, new_ref, pool_ref, o_ref, pages, keys, values, sem):
    step = pl.program_id(0)
    block = q_ref.shape[0]
    spare = new_ref.shape[0]

    @pl.when(step == 0)
    def _():
        for j in range(16):
            pltpu.make_async_copy(pool_ref.at[table[j], 0], pages.at[j], sem).start()
        new = new_ref[...]
        keys[spare:, :] = new[:, :HD]
        values[spare:, :HD] = new[:, HD:]
        values[spare:, HD:] = jnp.ones((spare, HD), jnp.bfloat16)
        pltpu.make_async_copy(pool_ref.at[pl.ds(0, 16), 0], pages, sem).wait()
        old = pages[...].reshape(16 * PAGE, 2 * HD).astype(jnp.float32)
        seen = lax.broadcasted_iota(jnp.int32, (16 * PAGE, HD), 0) < prefix[0]
        first = new[0:16, :HD].astype(jnp.float32)[0:1, :]
        keys[:spare, :] = jnp.where(seen, old[:, :HD], first).astype(jnp.bfloat16)
        values[:spare, :HD] = jnp.where(seen, old[:, HD:], 0.0).astype(jnp.bfloat16)
        values[:spare, HD:] = jnp.where(seen, 1.0, 0.0).astype(jnp.bfloat16)

    for case in range(spare // 256):

        @pl.when(step // 2 == case)
        def _(case=case):
            used = spare + 256 * (case + 1)
            row0 = (step % 2) * block

            @pl.loop(0, QPK // 2)
            def _(pair):
                c0 = pl.multiple_of(pair * 2 * HD, 2 * HD)
                c1 = pl.multiple_of(pair * 2 * HD + HD, HD)
                q = jnp.concatenate([q_ref[:, pl.ds(c0, HD)], q_ref[:, pl.ds(c1, HD)]], axis=0)
                out = attend_tile(q, keys[:used, :], values[:used, :], row0, block)
                out = out.astype(jnp.bfloat16)
                o_ref[:, pl.ds(c0, HD)] = out[:block]
                o_ref[:, pl.ds(c1, HD)] = out[block:]


def prefill(query_all, pair_all, pool, table, prefix):
    rows, width = query_all.shape
    block = 128
    spec = pl.BlockSpec((block, width), lambda i, t, p: (i, 0))
    return pl.pallas_call(
        prefill_kernel,
        out_shape=jax.ShapeDtypeStruct((rows, width), jnp.bfloat16),
        grid_spec=pltpu.PrefetchScalarGridSpec(
            num_scalar_prefetch=2,
            grid=(rows // block,),
            in_specs=[
                spec,
                pl.BlockSpec((rows, 2 * HD), lambda i, t, p: (0, 0)),
                pl.BlockSpec(memory_space=pl.ANY),
            ],
            out_specs=spec,
            scratch_shapes=[
                pltpu.VMEM((16, PAGE, 2 * HD), jnp.bfloat16),
                pltpu.VMEM((2 * rows, HD), jnp.bfloat16),
                pltpu.VMEM((2 * rows, 2 * HD), jnp.bfloat16),
                pltpu.SemaphoreType.DMA,
            ],
        ),
        compiler_params=pltpu.CompilerParams(
            dimension_semantics=("arbitrary",), vmem_limit_bytes=40 * 1024 * 1024
        ),
        cost_estimate=pl.CostEstimate(
            flops=2 * 8192 * 1600 * 384, bytes_accessed=6 << 20, transcendentals=8192 * 1600
        ),
        name="prefill_attention",
    )(table, prefix, query_all, pair_all, pool)


def decode_kernel(
    dtable, ptable, lengths, scalars, q_ref, pair_ref, mig_ref, new_ref, pool_ref, o_ref, out_ref,
    buf, in_sem, out_sem,
):
    slots = q_ref.shape[0]
    per_slot = buf.shape[1]

    @pl.loop(0, slots * per_slot)
    def _(n):
        s, j = n // per_slot, n % per_slot
        pltpu.make_async_copy(pool_ref.at[dtable[s, j], 0], buf.at[s, j], in_sem.at[s]).start()

    for part in range(2):

        @pl.loop(0, per_slot)
        def _(j, part=part):
            page = ptable[part * per_slot + j]
            pltpu.make_async_copy(
                pool_ref.at[page, 0], buf.at[slots + part, j], in_sem.at[slots + part]
            ).start()

    for s in range(slots):
        pltpu.make_async_copy(pool_ref.at[pl.ds(0, per_slot), 0], buf.at[s], in_sem.at[s]).wait()

        @pl.when(scalars[0] == s)
        def _(s=s):
            buf[s, 0:MIGP] = mig_ref[...]

        length = lengths[s]
        page, row = length // PAGE, length % PAGE
        base = pl.multiple_of((row // 16) * 16, 16)
        tile = buf[s, page, pl.ds(base, 16), :].astype(jnp.float32)
        hit = lax.broadcasted_iota(jnp.int32, tile.shape, 0) == row - base
        tile = jnp.where(hit, pair_ref[s : s + 1, :], tile)
        buf[s, page, pl.ds(base, 16), :] = tile.astype(jnp.bfloat16)

        @pl.loop(0, per_slot)
        def _(j, s=s):
            pltpu.make_async_copy(buf.at[s, j], out_ref.at[dtable[s, j], 0], out_sem.at[s]).start()

        kv = buf[s].reshape(per_slot * PAGE, 2 * HD)
        scores = lax.dot_general(q_ref[s], kv[:, :HD], NT, preferred_element_type=jnp.float32)
        seen = lax.broadcasted_iota(jnp.int32, scores.shape, 1) <= length
        scores = jnp.where(seen, scores, NEG)
        top = jnp.max(scores, axis=1, keepdims=True)
        weights = jnp.exp2((scores - top) * (HD**-0.5 * LOG2E))
        total = jnp.sum(weights, axis=1, keepdims=True)
        mixed = jnp.dot(weights.astype(jnp.bfloat16), kv[:, HD:], preferred_element_type=jnp.float32)
        o_ref[s] = (mixed / total).astype(jnp.bfloat16)

    first = scalars[1]
    for part in range(2):
        at = slots + part
        pltpu.make_async_copy(pool_ref.at[pl.ds(0, per_slot), 0], buf.at[at], in_sem.at[at]).wait()

        @pl.loop(0, per_slot)
        def _(j, part=part, at=at):
            logical = part * per_slot + j
            page = ptable[logical]
            fresh = jnp.logical_and(logical >= first, logical < first + 16)

            @pl.when(fresh)
            def _():
                pltpu.make_async_copy(
                    new_ref.at[logical - first], out_ref.at[page, 0], out_sem.at[at]
                ).start()

            @pl.when(jnp.logical_not(fresh))
            def _():
                pltpu.make_async_copy(buf.at[at, j], out_ref.at[page, 0], out_sem.at[at]).start()

    for at in range(slots + 2):
        pltpu.make_async_copy(buf.at[at], out_ref.at[pl.ds(0, per_slot), 0], out_sem.at[at]).wait()


def decode_and_store(query, pairs, arriving, pair_all, pool, dtable, ptable, lengths, scalars):
    slots, per_slot = dtable.shape
    vmem = pl.BlockSpec(memory_space=pltpu.VMEM)
    smem = pl.BlockSpec(memory_space=pltpu.SMEM)
    hbm = pl.BlockSpec(memory_space=pl.ANY)
    return pl.pallas_call(
        decode_kernel,
        out_shape=(
            jax.ShapeDtypeStruct(query.shape, jnp.bfloat16),
            jax.ShapeDtypeStruct(pool.shape, pool.dtype),
        ),
        in_specs=[smem] * 4 + [vmem] * 4 + [hbm],
        out_specs=(vmem, hbm),
        scratch_shapes=[
            pltpu.VMEM((slots + 2, per_slot, PAGE, 2 * HD), jnp.bfloat16),
            pltpu.SemaphoreType.DMA((slots + 2,)),
            pltpu.SemaphoreType.DMA((slots + 2,)),
        ],
        compiler_params=pltpu.CompilerParams(vmem_limit_bytes=24 * 1024 * 1024),
        cost_estimate=pl.CostEstimate(
            flops=2 * 64 * 1024 * 256, bytes_accessed=11 << 20, transcendentals=64 * 1024
        ),
        name="decode_and_pool",
    )(dtable, ptable, lengths, scalars, query, pairs, arriving, pair_all, pool)


def per_device(
    prefill_query,
    prefill_pairs,
    decode_query,
    decode_pairs,
    cache_pool,
    decode_pages,
    prefill_pages,
    cache_length,
    prefix_length,
    migrant_slot,
    migrant_target,
    arrivals,
):
    my_group = lax.axis_index("dp")
    my_z, my_x = my_group // NX, my_group % NX
    heads = lax.axis_size("head")
    groups = lax.axis_size("dp")
    nz = groups // NX
    slot_count = decode_pages.shape[0]
    along_x = [[z * NX + x for x in range(NX)] for z in range(nz)]
    along_z = [[z * NX + x for z in range(nz)] for x in range(NX)]

    tokens = jnp.concatenate(
        [decode_query.reshape(1, heads, QPK * HD), decode_pairs.reshape(1, heads, 2 * HD)], axis=2
    )
    tokens = lax.all_to_all(tokens, "head", split_axis=1, concat_axis=0, tiled=True)
    width = tokens.shape[2]
    pair_all = lax.all_to_all(prefill_pairs, "head", split_axis=1, concat_axis=0, tiled=True)
    query_all = lax.all_to_all(prefill_query, "head", split_axis=1, concat_axis=0, tiled=True)

    my_slot = migrant_slot[my_group, 0]
    own_pages = lax.dynamic_slice_in_dim(decode_pages, my_slot, 1)[0, :MIGP]
    leaving = cache_pool[own_pages]
    page_size = leaving.size
    parcel = jnp.concatenate([leaving.reshape(-1, 2 * HD), tokens.reshape(-1, 2 * HD)])
    page_rows = page_size // (2 * HD)
    row = lax.all_to_all(
        jnp.broadcast_to(parcel[None], (NX,) + parcel.shape),
        "dp", split_axis=0, concat_axis=0, tiled=True, axis_index_groups=along_x,
    )
    target = migrant_target[:, 0]
    row_target = lax.dynamic_slice_in_dim(target, my_z * NX, NX)
    want = jnp.arange(nz, dtype=jnp.int32) * NX + my_x
    pick = jnp.argmax((row_target[None, :] == want[:, None]).astype(jnp.int32), axis=1)
    chosen_pages = row[:, :page_rows][pick]
    row_tokens = row[:, page_rows:].reshape(NX * slot_count, width)
    row_slots = lax.dynamic_slice_in_dim(arrivals, my_z * NX * slot_count, NX * slot_count)
    want_slots = (want[:, None] * slot_count + jnp.arange(slot_count, dtype=jnp.int32)).reshape(-1)
    onehot = (want_slots[:, None] == row_slots[None, :]).astype(jnp.bfloat16)
    sorted_tokens = jnp.dot(onehot, row_tokens, preferred_element_type=jnp.float32)
    sorted_tokens = sorted_tokens.astype(jnp.bfloat16).reshape(nz, -1, 2 * HD)
    column = lax.all_to_all(
        jnp.concatenate([chosen_pages, sorted_tokens], axis=1),
        "dp", split_axis=0, concat_axis=0, tiled=True, axis_index_groups=along_z,
    )
    source = jnp.argmax((target == my_group).astype(jnp.int32)).astype(jnp.int32)
    arriving = lax.dynamic_index_in_dim(column[:, :page_rows], source // NX, keepdims=False)
    arriving = arriving.reshape(MIGP, PAGE, 2 * HD)
    my_tokens = jnp.sum(column[:, page_rows:].astype(jnp.float32), axis=0).reshape(slot_count, width)
    query_rows = my_tokens[:, : QPK * HD].astype(jnp.bfloat16).reshape(slot_count, QPK, HD)
    pair_rows = my_tokens[:, QPK * HD :]

    incoming = cache_length[source * slot_count + migrant_slot[source, 0]]
    own_len = lax.dynamic_slice_in_dim(cache_length, my_group * slot_count, slot_count)
    lengths = jnp.where(jnp.arange(slot_count, dtype=jnp.int32) == my_slot, incoming, own_len)

    table = prefill_pages[0]
    out_span = prefill(query_all, pair_all, cache_pool, table, prefix_length)
    prefill_attended = lax.all_to_all(out_span, "head", split_axis=0, concat_axis=1, tiled=True)
    scalars = jnp.stack([my_slot, prefix_length[0] // PAGE])
    decoded, new_pool = decode_and_store(
        query_rows, pair_rows, arriving, pair_all.reshape(-1, PAGE, 2 * HD), cache_pool,
        decode_pages, table, lengths, scalars,
    )
    return (prefill_attended, decoded.reshape(slot_count, -1), new_pool)


def solution(mesh):
    placed = (
        P(("dp", "head"), None),
        P(("dp", "head"), None),
        P(("dp", "head"), None),
        P(("dp", "head"), None),
        P("dp", "head", None, None),
        P("dp", None),
        P("dp", None),
        P(),
        P("dp"),
        P(),
        P(),
        P(),
    )
    return jax.shard_map(
        per_device,
        mesh=mesh,
        in_specs=placed,
        out_specs=(P(("dp", "head"), None), P("dp", "head"), P("dp", "head", None, None)),
        check_vma=False,
    )
```

```python
import jax
import jax.numpy as jnp
from jax import lax
from jax.experimental import pallas as pl
from jax.experimental.pallas import tpu as pltpu
from jax.sharding import PartitionSpec as P

HD = 128
PAGE = 64
MIGP = 4
QPK = 8
LOG2E = 1.4426950408889634
NEG = -1e30
NT = (((1,), (1,)), ((), ()))


def attend_tile(q, k, v, row0, mask_rows):
    keys = k.shape[0]
    scores = lax.dot_general(q, k, NT, preferred_element_type=jnp.float32)
    tail = scores[:, keys - 256 :]
    row = lax.broadcasted_iota(jnp.int32, tail.shape, 0) % mask_rows + row0
    col = lax.broadcasted_iota(jnp.int32, tail.shape, 1)
    tail = jnp.where(col <= row, tail, NEG)
    scores = jnp.concatenate([scores[:, : keys - 256], tail], axis=1)
    top = jnp.max(scores, axis=1, keepdims=True)
    weights = jnp.exp2((scores - top) * (HD**-0.5 * LOG2E)).astype(jnp.bfloat16)
    mixed = jnp.dot(weights, v, preferred_element_type=jnp.float32)
    return mixed[:, :HD] / mixed[:, HD : HD + 1]


def prefill_kernel(
    prefix, q_ref, pair_ref, tok_ref, leave_ref, old_ref,
    out_ref, pair_out, tok_out, mig_out,
    qbuf, pbuf, tbuf, obuf, keys, values,
    q_send, q_recv, p_send, p_recv, t_send, t_recv, o_send, o_recv,
    a_send, a_recv, m_send, m_recv,
):
    heads, block, width = qbuf.shape
    groups = mig_out.shape[0]
    spare = heads * block
    d = lax.axis_index("dp")
    h = lax.axis_index("head")
    chip, core = h // 2, h % 2
    chips = heads // 2

    def head_at(step, sign):
        ring = step // 2
        ring = ring + ring // 2 - 2 * (ring // 3)
        return ((chip + sign * ring + chips) % chips) * 2 + (core + step) % 2

    def cols(p, n):
        return pl.ds(pl.multiple_of(p * n, n), n)

    def to_head(src, dst, send, recv, p):
        return pltpu.make_async_remote_copy(
            src_ref=src, dst_ref=dst, send_sem=send.at[p], recv_sem=recv.at[h],
            device_id=(d, p), device_id_type=pl.DeviceIdType.MESH,
        )

    def to_group(src, dst, send, recv, g):
        return pltpu.make_async_remote_copy(
            src_ref=src, dst_ref=dst, send_sem=send.at[g], recv_sem=recv.at[d],
            device_id=(g, h), device_id_type=pl.DeviceIdType.MESH,
        )

    def landed(ref, sem):
        pltpu.make_async_copy(ref, ref, sem).wait()

    barrier = pltpu.get_barrier_semaphore()

    @pl.loop(1, heads)
    def _(k):
        pl.semaphore_signal(
            barrier, inc=1, device_id=(d, (h + k) % heads), device_id_type=pl.DeviceIdType.MESH
        )

    @pl.loop(1, groups)
    def _(k):
        pl.semaphore_signal(
            barrier, inc=1, device_id=((d + k) % groups, h), device_id_type=pl.DeviceIdType.MESH
        )

    pl.semaphore_wait(barrier, heads + groups - 2)

    pltpu.make_async_copy(tok_ref.at[h], tbuf.at[d, h], t_recv.at[h]).start()
    pltpu.make_async_copy(pair_ref.at[:, cols(h, 2 * HD)], pbuf.at[h], p_recv.at[h]).start()
    pltpu.make_async_copy(q_ref.at[:, cols(h, width)], qbuf.at[h], q_recv.at[h]).start()
    pltpu.make_async_copy(leave_ref, mig_out.at[d], m_recv.at[d]).start()

    @pl.loop(1, heads)
    def _(k):
        p = head_at(k, 1)
        to_head(tok_ref.at[p], tbuf.at[d, h], t_send, t_recv, p).start()
        to_head(pair_ref.at[:, cols(p, 2 * HD)], pbuf.at[h], p_send, p_recv, p).start()

    @pl.loop(1, heads)
    def _(k):
        p = head_at(k, 1)
        to_head(q_ref.at[:, cols(p, width)], qbuf.at[h], q_send, q_recv, p).start()

    @pl.loop(1, groups)
    def _(k):
        g = (d + k) % groups
        to_group(leave_ref, mig_out.at[d], m_send, m_recv, g).start()

    @pl.loop(0, heads)
    def _(p):
        landed(tbuf.at[d, p], t_recv.at[p])

    @pl.loop(1, groups)
    def _(k):
        g = (d + k) % groups
        to_group(tbuf.at[d], tbuf.at[d], a_send, a_recv, g).start()

    @pl.loop(0, heads)
    def _(p):
        landed(pbuf.at[p], p_recv.at[p])

    new = pbuf[...].reshape(spare, 2 * HD)
    pair_out[...] = new
    keys[spare:, :] = new[:, :HD]
    values[spare:, :HD] = new[:, HD:]
    values[spare:, HD:] = jnp.ones((spare, HD), jnp.bfloat16)
    old = old_ref[...].astype(jnp.float32)
    seen = lax.broadcasted_iota(jnp.int32, (spare, HD), 0) < prefix[0]
    first = new[0:16, :HD].astype(jnp.float32)[0:1, :]
    keys[:spare, :] = jnp.where(seen, old[:, :HD], first).astype(jnp.bfloat16)
    values[:spare, :HD] = jnp.where(seen, old[:, HD:], 0.0).astype(jnp.bfloat16)
    values[:spare, HD:] = jnp.where(seen, 1.0, 0.0).astype(jnp.bfloat16)

    @pl.loop(0, heads)
    def _(step):
        src = head_at(step, -1)
        landed(qbuf.at[src], q_recv.at[src])
        for case in range(spare // 256):

            @pl.when(src // 2 == case)
            def _(case=case):
                used = spare + 256 * (case + 1)
                row0 = (src % 2) * block

                @pl.loop(0, QPK // 2)
                def _(pair):
                    c0 = pl.multiple_of(pair * 2 * HD, 2 * HD)
                    c1 = pl.multiple_of(pair * 2 * HD + HD, HD)
                    q = jnp.concatenate(
                        [qbuf[src, :, pl.ds(c0, HD)], qbuf[src, :, pl.ds(c1, HD)]], axis=0
                    )
                    out = attend_tile(q, keys[:used, :], values[:used, :], row0, block)
                    out = out.astype(jnp.bfloat16)
                    obuf[src, :, pl.ds(c0, HD)] = out[:block]
                    obuf[src, :, pl.ds(c1, HD)] = out[block:]

        @pl.when(step == 0)
        def _():
            pltpu.make_async_copy(obuf.at[h], out_ref.at[:, cols(h, width)], o_recv.at[h]).start()

        @pl.when(step > 0)
        def _():
            to_head(obuf.at[src], out_ref.at[:, cols(h, width)], o_send, o_recv, src).start()

    @pl.loop(1, groups)
    def _(k):
        g = (d + k) % groups
        landed(tbuf.at[g], a_recv.at[g])
        landed(tbuf.at[d], a_send.at[g])
        landed(mig_out.at[g], m_recv.at[g])
        landed(leave_ref, m_send.at[g])

    landed(mig_out.at[d], m_recv.at[d])
    tok_out[...] = tbuf[...]

    @pl.loop(1, heads)
    def _(k):
        p = (h + k) % heads
        landed(tok_ref.at[p], t_send.at[p])
        landed(pbuf.at[p], p_send.at[p])
        landed(qbuf.at[p], q_send.at[p])
        landed(obuf.at[p], o_send.at[p])

    @pl.loop(0, heads)
    def _(p):
        landed(out_ref.at[:, cols(p, width)], o_recv.at[p])


def prefill(prefix, query, pairs, tokens, leaving, old, heads, groups):
    block, columns = query.shape
    width = columns // heads
    rows = block * heads
    bf16 = jnp.bfloat16
    vmem = pl.BlockSpec(memory_space=pltpu.VMEM)
    hbm = pl.BlockSpec(memory_space=pl.ANY)
    sem = pltpu.SemaphoreType.DMA
    return pl.pallas_call(
        prefill_kernel,
        out_shape=(
            jax.ShapeDtypeStruct((block, columns), bf16),
            jax.ShapeDtypeStruct((rows, 2 * HD), bf16),
            jax.ShapeDtypeStruct((groups,) + tokens.shape, bf16),
            jax.ShapeDtypeStruct((groups,) + leaving.shape, bf16),
        ),
        in_specs=[pl.BlockSpec(memory_space=pltpu.SMEM), hbm, hbm, vmem, vmem, vmem],
        out_specs=(hbm, vmem, vmem, hbm),
        scratch_shapes=[
            pltpu.VMEM((heads, block, width), bf16),
            pltpu.VMEM((heads, block, 2 * HD), bf16),
            pltpu.VMEM((groups,) + tokens.shape, bf16),
            pltpu.VMEM((heads, block, width), bf16),
            pltpu.VMEM((2 * rows, HD), bf16),
            pltpu.VMEM((2 * rows, 2 * HD), bf16),
        ]
        + [sem((heads,))] * 8
        + [sem((groups,))] * 4,
        compiler_params=pltpu.CompilerParams(
            collective_id=0, has_side_effects=True, vmem_limit_bytes=44 * 1024 * 1024
        ),
        name="prefill_exchange",
    )(prefix, query, pairs, tokens, leaving, old)


def decode_kernel(
    dtable, ptable, lengths, scalars, q_ref, pair_ref, mig_ref, new_ref, pool_ref, o_ref, out_ref,
    buf, in_sem, out_sem,
):
    slots = q_ref.shape[0]
    per_slot = buf.shape[1]

    @pl.loop(0, slots * per_slot)
    def _(n):
        s, j = n // per_slot, n % per_slot
        pltpu.make_async_copy(pool_ref.at[dtable[s, j], 0], buf.at[s, j], in_sem.at[s]).start()

    for part in range(2):

        @pl.loop(0, per_slot)
        def _(j, part=part):
            page = ptable[part * per_slot + j]
            pltpu.make_async_copy(
                pool_ref.at[page, 0], buf.at[slots + part, j], in_sem.at[slots + part]
            ).start()

    for s in range(slots):
        pltpu.make_async_copy(pool_ref.at[pl.ds(0, per_slot), 0], buf.at[s], in_sem.at[s]).wait()

        @pl.when(scalars[0] == s)
        def _(s=s):
            buf[s, 0:MIGP] = mig_ref[...]

        length = lengths[s]
        page, row = length // PAGE, length % PAGE
        base = pl.multiple_of((row // 16) * 16, 16)
        tile = buf[s, page, pl.ds(base, 16), :].astype(jnp.float32)
        hit = lax.broadcasted_iota(jnp.int32, tile.shape, 0) == row - base
        tile = jnp.where(hit, pair_ref[s : s + 1, :], tile)
        buf[s, page, pl.ds(base, 16), :] = tile.astype(jnp.bfloat16)

        @pl.loop(0, per_slot)
        def _(j, s=s):
            pltpu.make_async_copy(buf.at[s, j], out_ref.at[dtable[s, j], 0], out_sem.at[s]).start()

        kv = buf[s].reshape(per_slot * PAGE, 2 * HD)
        scores = lax.dot_general(q_ref[s], kv[:, :HD], NT, preferred_element_type=jnp.float32)
        seen = lax.broadcasted_iota(jnp.int32, scores.shape, 1) <= length
        scores = jnp.where(seen, scores, NEG)
        top = jnp.max(scores, axis=1, keepdims=True)
        weights = jnp.exp2((scores - top) * (HD**-0.5 * LOG2E))
        total = jnp.sum(weights, axis=1, keepdims=True)
        mixed = jnp.dot(weights.astype(jnp.bfloat16), kv[:, HD:], preferred_element_type=jnp.float32)
        o_ref[s] = (mixed / total).astype(jnp.bfloat16)

    first = scalars[1]
    for part in range(2):
        at = slots + part
        pltpu.make_async_copy(pool_ref.at[pl.ds(0, per_slot), 0], buf.at[at], in_sem.at[at]).wait()

        @pl.loop(0, per_slot)
        def _(j, part=part, at=at):
            logical = part * per_slot + j
            page = ptable[logical]
            fresh = jnp.logical_and(logical >= first, logical < first + 16)

            @pl.when(fresh)
            def _():
                pltpu.make_async_copy(
                    new_ref.at[logical - first], out_ref.at[page, 0], out_sem.at[at]
                ).start()

            @pl.when(jnp.logical_not(fresh))
            def _():
                pltpu.make_async_copy(buf.at[at, j], out_ref.at[page, 0], out_sem.at[at]).start()

    for at in range(slots + 2):
        pltpu.make_async_copy(buf.at[at], out_ref.at[pl.ds(0, per_slot), 0], out_sem.at[at]).wait()


def decode_and_store(query, pairs, arriving, pair_all, pool, dtable, ptable, lengths, scalars):
    slots, per_slot = dtable.shape
    vmem = pl.BlockSpec(memory_space=pltpu.VMEM)
    smem = pl.BlockSpec(memory_space=pltpu.SMEM)
    hbm = pl.BlockSpec(memory_space=pl.ANY)
    return pl.pallas_call(
        decode_kernel,
        out_shape=(
            jax.ShapeDtypeStruct(query.shape, jnp.bfloat16),
            jax.ShapeDtypeStruct(pool.shape, pool.dtype),
        ),
        in_specs=[smem] * 4 + [vmem] * 4 + [hbm],
        out_specs=(vmem, hbm),
        scratch_shapes=[
            pltpu.VMEM((slots + 2, per_slot, PAGE, 2 * HD), jnp.bfloat16),
            pltpu.SemaphoreType.DMA((slots + 2,)),
            pltpu.SemaphoreType.DMA((slots + 2,)),
        ],
        compiler_params=pltpu.CompilerParams(vmem_limit_bytes=24 * 1024 * 1024),
        cost_estimate=pl.CostEstimate(
            flops=2 * 64 * 1024 * 256, bytes_accessed=11 << 20, transcendentals=64 * 1024
        ),
        name="decode_and_pool",
    )(dtable, ptable, lengths, scalars, query, pairs, arriving, pair_all, pool)


def per_device(
    prefill_query,
    prefill_pairs,
    decode_query,
    decode_pairs,
    cache_pool,
    decode_pages,
    prefill_pages,
    cache_length,
    prefix_length,
    migrant_slot,
    migrant_target,
    arrivals,
):
    my_group = lax.axis_index("dp")
    heads = lax.axis_size("head")
    groups = lax.axis_size("dp")
    slot_count = decode_pages.shape[0]

    my_slot = migrant_slot[my_group, 0]
    own_pages = lax.dynamic_slice_in_dim(decode_pages, my_slot, 1)[0, :MIGP]
    table = prefill_pages[0]
    picked = cache_pool[jnp.concatenate([own_pages, table[: 1024 // PAGE]]), 0]
    leaving = picked[:MIGP].reshape(-1, 2 * HD)
    old = picked[MIGP:].reshape(-1, 2 * HD)
    tokens = jnp.concatenate(
        [
            decode_query.reshape(heads, QPK, HD),
            decode_pairs.reshape(heads, 2, HD),
            jnp.zeros((heads, 6, HD), jnp.bfloat16),
        ],
        axis=1,
    )
    prefill_attended, pair_all, all_tokens, all_leaving = prefill(
        prefix_length, prefill_query, prefill_pairs, tokens, leaving, old, heads, groups
    )

    source = jnp.argmax((migrant_target[:, 0] == my_group).astype(jnp.int32)).astype(jnp.int32)
    arriving = lax.dynamic_index_in_dim(all_leaving, source, keepdims=False)
    arriving = arriving.reshape(MIGP, PAGE, 2 * HD)
    wanted = my_group * slot_count + jnp.arange(slot_count, dtype=jnp.int32)
    onehot = (wanted[:, None] == arrivals[None, :]).astype(jnp.bfloat16)
    my_tokens = jnp.dot(
        onehot, all_tokens.reshape(groups * slot_count, -1), preferred_element_type=jnp.float32
    )
    query_rows = my_tokens[:, : QPK * HD].astype(jnp.bfloat16).reshape(slot_count, QPK, HD)
    pair_rows = my_tokens[:, QPK * HD : (QPK + 2) * HD]

    incoming = cache_length[source * slot_count + migrant_slot[source, 0]]
    own_len = lax.dynamic_slice_in_dim(cache_length, my_group * slot_count, slot_count)
    lengths = jnp.where(jnp.arange(slot_count, dtype=jnp.int32) == my_slot, incoming, own_len)

    scalars = jnp.stack([my_slot, prefix_length[0] // PAGE])
    decoded, new_pool = decode_and_store(
        query_rows, pair_rows, arriving, pair_all.reshape(-1, PAGE, 2 * HD), cache_pool,
        decode_pages, table, lengths, scalars,
    )
    return (prefill_attended, decoded.reshape(slot_count, -1), new_pool)


def solution(mesh):
    placed = (
        P(("dp", "head"), None),
        P(("dp", "head"), None),
        P(("dp", "head"), None),
        P(("dp", "head"), None),
        P("dp", "head", None, None),
        P("dp", None),
        P("dp", None),
        P(),
        P("dp"),
        P(),
        P(),
        P(),
    )
    return jax.shard_map(
        per_device,
        mesh=mesh,
        in_specs=placed,
        out_specs=(P(("dp", "head"), None), P("dp", "head"), P("dp", "head", None, None)),
        check_vma=False,
    )
```

```python
import jax
import jax.numpy as jnp
from jax import lax
from jax.experimental import pallas as pl
from jax.experimental.pallas import tpu as pltpu
from jax.sharding import PartitionSpec as P

HD = 128
PAGE = 64
MIGP = 4
QPK = 8
LOG2E = 1.4426950408889634
NEG = -1e30
NT = (((1,), (1,)), ((), ()))


def attend_tile(q, k, v, row0, mask_rows):
    keys = k.shape[0]
    scores = lax.dot_general(q, k, NT, preferred_element_type=jnp.float32)
    tail = scores[:, keys - 256 :]
    row = lax.broadcasted_iota(jnp.int32, tail.shape, 0) % mask_rows + row0
    col = lax.broadcasted_iota(jnp.int32, tail.shape, 1)
    tail = jnp.where(col <= row, tail, NEG)
    scores = jnp.concatenate([scores[:, : keys - 256], tail], axis=1)
    top = jnp.max(scores, axis=1, keepdims=True)
    weights = jnp.exp2((scores - top) * (HD**-0.5 * LOG2E)).astype(jnp.bfloat16)
    mixed = jnp.dot(weights, v, preferred_element_type=jnp.float32)
    return mixed[:, :HD] / mixed[:, HD : HD + 1]


def prefill_kernel(
    prefix, q_ref, pair_ref, tok_ref, leave_ref, old_ref,
    out_ref, pair_out, tok_out, mig_out,
    qbuf, pbuf, tbuf, obuf, keys, values,
    q_send, q_recv, p_send, p_recv, t_send, t_recv, o_send, o_recv,
    a_send, a_recv, m_send, m_recv,
):
    heads, block, width = qbuf.shape
    groups = mig_out.shape[0]
    spare = heads * block
    d = lax.axis_index("dp")
    h = lax.axis_index("head")
    chip, core = h // 2, h % 2
    chips = heads // 2

    def head_at(step, sign):
        ring = step // 2
        ring = ring + ring // 2 - 2 * (ring // 3)
        return ((chip + sign * ring + chips) % chips) * 2 + (core + step) % 2

    def cols(p, n):
        return pl.ds(pl.multiple_of(p * n, n), n)

    def to_head(src, dst, send, recv, p):
        return pltpu.make_async_remote_copy(
            src_ref=src, dst_ref=dst, send_sem=send.at[p], recv_sem=recv.at[h],
            device_id=(d, p), device_id_type=pl.DeviceIdType.MESH,
        )

    def to_group(src, dst, send, recv, g):
        return pltpu.make_async_remote_copy(
            src_ref=src, dst_ref=dst, send_sem=send.at[g], recv_sem=recv.at[d],
            device_id=(g, h), device_id_type=pl.DeviceIdType.MESH,
        )

    def landed(ref, sem):
        pltpu.make_async_copy(ref, ref, sem).wait()

    barrier = pltpu.get_barrier_semaphore()

    @pl.loop(1, heads)
    def _(k):
        pl.semaphore_signal(
            barrier, inc=1, device_id=(d, (h + k) % heads), device_id_type=pl.DeviceIdType.MESH
        )

    @pl.loop(1, groups)
    def _(k):
        pl.semaphore_signal(
            barrier, inc=1, device_id=((d + k) % groups, h), device_id_type=pl.DeviceIdType.MESH
        )

    pl.semaphore_wait(barrier, heads + groups - 2)

    pltpu.make_async_copy(tok_ref.at[h], tbuf.at[d, h], t_recv.at[h]).start()
    pltpu.make_async_copy(pair_ref.at[:, cols(h, 2 * HD)], pbuf.at[h], p_recv.at[h]).start()
    pltpu.make_async_copy(q_ref.at[:, cols(h, width)], qbuf.at[h], q_recv.at[h]).start()
    pltpu.make_async_copy(leave_ref, mig_out.at[d], m_recv.at[d]).start()

    @pl.loop(1, heads)
    def _(k):
        p = head_at(k, 1)
        to_head(tok_ref.at[p], tbuf.at[d, h], t_send, t_recv, p).start()
        to_head(pair_ref.at[:, cols(p, 2 * HD)], pbuf.at[h], p_send, p_recv, p).start()

    @pl.loop(1, heads)
    def _(k):
        p = head_at(k, 1)
        to_head(q_ref.at[:, cols(p, width)], qbuf.at[h], q_send, q_recv, p).start()

    @pl.loop(1, groups)
    def _(k):
        g = (d + k) % groups
        to_group(leave_ref, mig_out.at[d], m_send, m_recv, g).start()

    @pl.loop(0, heads)
    def _(p):
        landed(tbuf.at[d, p], t_recv.at[p])

    @pl.loop(1, groups)
    def _(k):
        g = (d + k) % groups
        to_group(tbuf.at[d], tbuf.at[d], a_send, a_recv, g).start()

    @pl.loop(0, heads)
    def _(p):
        landed(pbuf.at[p], p_recv.at[p])

    new = pbuf[...].reshape(spare, 2 * HD)
    pair_out[...] = new
    keys[spare:, :] = new[:, :HD]
    values[spare:, :HD] = new[:, HD:]
    values[spare:, HD:] = jnp.ones((spare, HD), jnp.bfloat16)
    old = old_ref[...].astype(jnp.float32)
    seen = lax.broadcasted_iota(jnp.int32, (spare, HD), 0) < prefix[0]
    first = new[0:16, :HD].astype(jnp.float32)[0:1, :]
    keys[:spare, :] = jnp.where(seen, old[:, :HD], first).astype(jnp.bfloat16)
    values[:spare, :HD] = jnp.where(seen, old[:, HD:], 0.0).astype(jnp.bfloat16)
    values[:spare, HD:] = jnp.where(seen, 1.0, 0.0).astype(jnp.bfloat16)

    @pl.loop(0, heads)
    def _(step):
        src = head_at(step, -1)
        landed(qbuf.at[src], q_recv.at[src])
        for case in range(spare // 256):

            @pl.when(src // 2 == case)
            def _(case=case):
                used = spare + 256 * (case + 1)
                row0 = (src % 2) * block

                @pl.loop(0, QPK // 2)
                def _(pair):
                    c0 = pl.multiple_of(pair * 2 * HD, 2 * HD)
                    c1 = pl.multiple_of(pair * 2 * HD + HD, HD)
                    q = jnp.concatenate(
                        [qbuf[src, :, pl.ds(c0, HD)], qbuf[src, :, pl.ds(c1, HD)]], axis=0
                    )
                    out = attend_tile(q, keys[:used, :], values[:used, :], row0, block)
                    out = out.astype(jnp.bfloat16)
                    obuf[src, :, pl.ds(c0, HD)] = out[:block]
                    obuf[src, :, pl.ds(c1, HD)] = out[block:]

        @pl.when(step == 0)
        def _():
            pltpu.make_async_copy(obuf.at[h], out_ref.at[:, cols(h, width)], o_recv.at[h]).start()

        @pl.when(step > 0)
        def _():
            to_head(obuf.at[src], out_ref.at[:, cols(h, width)], o_send, o_recv, src).start()

    @pl.loop(1, groups)
    def _(k):
        g = (d + k) % groups
        landed(tbuf.at[g], a_recv.at[g])
        landed(tbuf.at[d], a_send.at[g])
        landed(mig_out.at[g], m_recv.at[g])
        landed(leave_ref, m_send.at[g])

    landed(mig_out.at[d], m_recv.at[d])
    tok_out[...] = tbuf[...]

    @pl.loop(1, heads)
    def _(k):
        p = (h + k) % heads
        landed(tok_ref.at[p], t_send.at[p])
        landed(pbuf.at[p], p_send.at[p])
        landed(qbuf.at[p], q_send.at[p])
        landed(obuf.at[p], o_send.at[p])

    @pl.loop(0, heads)
    def _(p):
        landed(out_ref.at[:, cols(p, width)], o_recv.at[p])


def prefill(prefix, query, pairs, tokens, leaving, old, heads, groups):
    block, columns = query.shape
    width = columns // heads
    rows = block * heads
    bf16 = jnp.bfloat16
    vmem = pl.BlockSpec(memory_space=pltpu.VMEM)
    hbm = pl.BlockSpec(memory_space=pl.ANY)
    sem = pltpu.SemaphoreType.DMA
    return pl.pallas_call(
        prefill_kernel,
        out_shape=(
            jax.ShapeDtypeStruct((block, columns), bf16),
            jax.ShapeDtypeStruct((rows, 2 * HD), bf16),
            jax.ShapeDtypeStruct((groups,) + tokens.shape, bf16),
            jax.ShapeDtypeStruct((groups,) + leaving.shape, bf16),
        ),
        in_specs=[pl.BlockSpec(memory_space=pltpu.SMEM), hbm, hbm, vmem, vmem, vmem],
        out_specs=(hbm, vmem, vmem, hbm),
        scratch_shapes=[
            pltpu.VMEM((heads, block, width), bf16),
            pltpu.VMEM((heads, block, 2 * HD), bf16),
            pltpu.VMEM((groups,) + tokens.shape, bf16),
            pltpu.VMEM((heads, block, width), bf16),
            pltpu.VMEM((2 * rows, HD), bf16),
            pltpu.VMEM((2 * rows, 2 * HD), bf16),
        ]
        + [sem((heads,))] * 8
        + [sem((groups,))] * 4,
        compiler_params=pltpu.CompilerParams(
            collective_id=0, has_side_effects=True, vmem_limit_bytes=44 * 1024 * 1024
        ),
        name="prefill_exchange",
    )(prefix, query, pairs, tokens, leaving, old)


def gather_kernel(where, dtable, ptable, migrant, pool_ref, leave_ref, old_ref, sem):
    slot = migrant[where[0], 0]
    for j in range(leave_ref.shape[0]):
        pltpu.make_async_copy(pool_ref.at[dtable[slot, j], 0], leave_ref.at[j], sem.at[0]).start()
    for j in range(old_ref.shape[0]):
        pltpu.make_async_copy(pool_ref.at[ptable[0, j], 0], old_ref.at[j], sem.at[1]).start()
    for k, ref in enumerate((leave_ref, old_ref)):
        pltpu.make_async_copy(pool_ref.at[pl.ds(0, ref.shape[0]), 0], ref, sem.at[k]).wait()


def gather(where, dtable, ptable, migrant, pool, prefix_pages):
    vmem = pl.BlockSpec(memory_space=pltpu.VMEM)
    smem = pl.BlockSpec(memory_space=pltpu.SMEM)
    return pl.pallas_call(
        gather_kernel,
        out_shape=tuple(
            jax.ShapeDtypeStruct((n, PAGE, 2 * HD), pool.dtype) for n in (MIGP, prefix_pages)
        ),
        in_specs=[smem] * 4 + [pl.BlockSpec(memory_space=pl.ANY)],
        out_specs=(vmem, vmem),
        scratch_shapes=[pltpu.SemaphoreType.DMA((2,))],
        name="gather_pages",
    )(where, dtable, ptable, migrant, pool)


def decode_kernel(
    where, dtable, ptable, cached, migrant, target, prefix, arrivals,
    tok_ref, mig_ref, new_ref, pool_ref, o_ref, out_ref,
    buf, rows, in_sem, out_sem,
):
    slots = o_ref.shape[0]
    per_slot = buf.shape[1]
    group = where[0]
    my_slot = migrant[group, 0]
    source = lax.fori_loop(
        0, target.shape[0], lambda i, found: jnp.where(target[i, 0] == group, i, found), 0
    )
    incoming = cached[source * slots + migrant[source, 0]]

    @pl.loop(0, slots * per_slot)
    def _(n):
        s, j = n // per_slot, n % per_slot
        moved = jnp.logical_and(s == my_slot, j < MIGP)

        @pl.when(moved)
        def _():
            pltpu.make_async_copy(
                mig_ref.at[source, jnp.minimum(j, MIGP - 1)], buf.at[s, j], in_sem.at[s]
            ).start()

        @pl.when(jnp.logical_not(moved))
        def _():
            pltpu.make_async_copy(pool_ref.at[dtable[s, j], 0], buf.at[s, j], in_sem.at[s]).start()

    for part in range(2):

        @pl.loop(0, per_slot)
        def _(j, part=part):
            page = ptable[0, part * per_slot + j]
            pltpu.make_async_copy(
                pool_ref.at[page, 0], buf.at[slots + part, j], in_sem.at[slots + part]
            ).start()

    @pl.loop(0, arrivals.shape[0])
    def _(i):
        slot = arrivals[i]

        @pl.when(slot // slots == group)
        def _():
            rows[slot % slots] = i

    for s in range(slots):
        pltpu.make_async_copy(pool_ref.at[pl.ds(0, per_slot), 0], buf.at[s], in_sem.at[s]).wait()

        token = tok_ref[rows[s]]
        wide = token.astype(jnp.float32)
        pair = jnp.concatenate([wide[QPK : QPK + 1], wide[QPK + 1 : QPK + 2]], axis=1)
        length = jnp.where(my_slot == s, incoming, cached[group * slots + s])
        page, row = length // PAGE, length % PAGE
        base = pl.multiple_of((row // 16) * 16, 16)
        tile = buf[s, page, pl.ds(base, 16), :].astype(jnp.float32)
        hit = lax.broadcasted_iota(jnp.int32, tile.shape, 0) == row - base
        tile = jnp.where(hit, pair, tile)
        buf[s, page, pl.ds(base, 16), :] = tile.astype(jnp.bfloat16)

        @pl.loop(0, per_slot)
        def _(j, s=s):
            pltpu.make_async_copy(buf.at[s, j], out_ref.at[dtable[s, j], 0], out_sem.at[s]).start()

        kv = buf[s].reshape(per_slot * PAGE, 2 * HD)
        scores = lax.dot_general(token, kv[:, :HD], NT, preferred_element_type=jnp.float32)
        seen = lax.broadcasted_iota(jnp.int32, scores.shape, 1) <= length
        scores = jnp.where(seen, scores, NEG)
        top = jnp.max(scores, axis=1, keepdims=True)
        weights = jnp.exp2((scores - top) * (HD**-0.5 * LOG2E))
        total = jnp.sum(weights, axis=1, keepdims=True)
        mixed = jnp.dot(weights.astype(jnp.bfloat16), kv[:, HD:], preferred_element_type=jnp.float32)
        o_ref[s] = (mixed / total)[:QPK].astype(jnp.bfloat16)

    first = prefix[0] // PAGE
    for part in range(2):
        at = slots + part
        pltpu.make_async_copy(pool_ref.at[pl.ds(0, per_slot), 0], buf.at[at], in_sem.at[at]).wait()

        @pl.loop(0, per_slot)
        def _(j, part=part, at=at):
            logical = part * per_slot + j
            page = ptable[0, logical]
            fresh = jnp.logical_and(logical >= first, logical < first + 16)

            @pl.when(fresh)
            def _():
                pltpu.make_async_copy(
                    new_ref.at[logical - first], out_ref.at[page, 0], out_sem.at[at]
                ).start()

            @pl.when(jnp.logical_not(fresh))
            def _():
                pltpu.make_async_copy(buf.at[at, j], out_ref.at[page, 0], out_sem.at[at]).start()

    for at in range(slots + 2):
        pltpu.make_async_copy(buf.at[at], out_ref.at[pl.ds(0, per_slot), 0], out_sem.at[at]).wait()


def decode_and_store(
    where, dtable, ptable, cached, migrant, target, prefix, arrivals, tokens, moved, pair_all, pool
):
    slots, per_slot = dtable.shape
    vmem = pl.BlockSpec(memory_space=pltpu.VMEM)
    smem = pl.BlockSpec(memory_space=pltpu.SMEM)
    hbm = pl.BlockSpec(memory_space=pl.ANY)
    return pl.pallas_call(
        decode_kernel,
        out_shape=(
            jax.ShapeDtypeStruct((slots, QPK, HD), jnp.bfloat16),
            jax.ShapeDtypeStruct(pool.shape, pool.dtype),
        ),
        in_specs=[smem] * 8 + [vmem, hbm, vmem, hbm],
        out_specs=(vmem, hbm),
        scratch_shapes=[
            pltpu.VMEM((slots + 2, per_slot, PAGE, 2 * HD), jnp.bfloat16),
            pltpu.SMEM((slots,), jnp.int32),
            pltpu.SemaphoreType.DMA((slots + 2,)),
            pltpu.SemaphoreType.DMA((slots + 2,)),
        ],
        compiler_params=pltpu.CompilerParams(vmem_limit_bytes=24 * 1024 * 1024),
        cost_estimate=pl.CostEstimate(
            flops=2 * 64 * 1024 * 256, bytes_accessed=11 << 20, transcendentals=64 * 1024
        ),
        name="decode_and_pool",
    )(
        where, dtable, ptable, cached, migrant, target, prefix, arrivals, tokens, moved, pair_all,
        pool,
    )


def per_device(
    prefill_query,
    prefill_pairs,
    decode_query,
    decode_pairs,
    cache_pool,
    decode_pages,
    prefill_pages,
    cache_length,
    prefix_length,
    migrant_slot,
    migrant_target,
    arrivals,
):
    where = lax.axis_index("dp").astype(jnp.int32).reshape(1)
    heads = lax.axis_size("head")
    groups = lax.axis_size("dp")
    slot_count = decode_pages.shape[0]
    prefix_pages = prefill_pages.shape[1] // 2

    leaving, old = gather(
        where, decode_pages, prefill_pages, migrant_slot, cache_pool, prefix_pages
    )
    leaving = leaving.reshape(-1, 2 * HD)
    old = old.reshape(-1, 2 * HD)
    tokens = jnp.concatenate(
        [
            decode_query.reshape(heads, QPK, HD),
            decode_pairs.reshape(heads, 2, HD),
            jnp.zeros((heads, 6, HD), jnp.bfloat16),
        ],
        axis=1,
    )
    prefill_attended, pair_all, all_tokens, all_leaving = prefill(
        prefix_length, prefill_query, prefill_pairs, tokens, leaving, old, heads, groups
    )

    decoded, new_pool = decode_and_store(
        where, decode_pages, prefill_pages, cache_length, migrant_slot, migrant_target,
        prefix_length, arrivals, all_tokens.reshape(groups * slot_count, -1, HD),
        all_leaving.reshape(groups, MIGP, PAGE, 2 * HD), pair_all.reshape(-1, PAGE, 2 * HD),
        cache_pool,
    )
    return (prefill_attended, decoded.reshape(slot_count, -1), new_pool)


def solution(mesh):
    placed = (
        P(("dp", "head"), None),
        P(("dp", "head"), None),
        P(("dp", "head"), None),
        P(("dp", "head"), None),
        P("dp", "head", None, None),
        P("dp", None),
        P("dp", None),
        P(),
        P("dp"),
        P(),
        P(),
        P(),
    )
    return jax.shard_map(
        per_device,
        mesh=mesh,
        in_specs=placed,
        out_specs=(P(("dp", "head"), None), P("dp", "head"), P("dp", "head", None, None)),
        check_vma=False,
    )
```

```python
import jax
import jax.numpy as jnp
from jax import lax
from jax.experimental import pallas as pl
from jax.experimental.pallas import tpu as pltpu
from jax.sharding import PartitionSpec as P

HD = 128
PAGE = 64
MIGP = 4
QPK = 8
LOG2E = 1.4426950408889634
NEG = -1e30
NT = (((1,), (1,)), ((), ()))


def attend_tile(q, k, v, row0, mask_rows):
    keys = k.shape[0]
    scores = lax.dot_general(q, k, NT, preferred_element_type=jnp.float32)
    tail = scores[:, keys - 256 :]
    row = lax.broadcasted_iota(jnp.int32, tail.shape, 0) % mask_rows + row0
    col = lax.broadcasted_iota(jnp.int32, tail.shape, 1)
    tail = jnp.where(col <= row, tail, NEG)
    scores = jnp.concatenate([scores[:, : keys - 256], tail], axis=1)
    top = jnp.max(scores, axis=1, keepdims=True)
    weights = jnp.exp2((scores - top) * (HD**-0.5 * LOG2E)).astype(jnp.bfloat16)
    mixed = jnp.dot(weights, v, preferred_element_type=jnp.float32)
    return mixed[:, :HD] / mixed[:, HD : HD + 1]


def prefill_kernel(
    prefix, q_ref, pair_ref, tok_ref, leave_ref, old_ref,
    out_ref, pair_out, tok_out, mig_out,
    qbuf, pbuf, tbuf, obuf, keys, values,
    q_send, q_recv, p_send, p_recv, t_send, t_recv, o_send, o_recv,
    a_send, a_recv, m_send, m_recv,
):
    heads, block, width = qbuf.shape
    groups = mig_out.shape[0]
    spare = heads * block
    d = lax.axis_index("dp")
    h = lax.axis_index("head")
    chip, core = h // 2, h % 2
    chips = heads // 2

    def head_at(step, sign):
        ring = step // 2
        ring = ring + ring // 2 - 2 * (ring // 3)
        return ((chip + sign * ring + chips) % chips) * 2 + (core + step) % 2

    def cols(p, n):
        return pl.ds(pl.multiple_of(p * n, n), n)

    def to_head(src, dst, send, recv, p):
        return pltpu.make_async_remote_copy(
            src_ref=src, dst_ref=dst, send_sem=send.at[p], recv_sem=recv.at[h],
            device_id=(d, p), device_id_type=pl.DeviceIdType.MESH,
        )

    def to_group(src, dst, send, recv, g):
        return pltpu.make_async_remote_copy(
            src_ref=src, dst_ref=dst, send_sem=send.at[g], recv_sem=recv.at[d],
            device_id=(g, h), device_id_type=pl.DeviceIdType.MESH,
        )

    def landed(ref, sem):
        pltpu.make_async_copy(ref, ref, sem).wait()

    barrier = pltpu.get_barrier_semaphore()

    @pl.loop(1, heads)
    def _(k):
        pl.semaphore_signal(
            barrier, inc=1, device_id=(d, (h + k) % heads), device_id_type=pl.DeviceIdType.MESH
        )

    @pl.loop(1, groups)
    def _(k):
        pl.semaphore_signal(
            barrier, inc=1, device_id=((d + k) % groups, h), device_id_type=pl.DeviceIdType.MESH
        )

    pl.semaphore_wait(barrier, heads + groups - 2)

    pltpu.make_async_copy(tok_ref.at[h], tbuf.at[d, h], t_recv.at[h]).start()
    pltpu.make_async_copy(pair_ref.at[:, cols(h, 2 * HD)], pbuf.at[h], p_recv.at[h]).start()
    pltpu.make_async_copy(q_ref.at[:, cols(h, width)], qbuf.at[h], q_recv.at[h]).start()
    pltpu.make_async_copy(leave_ref, mig_out.at[d], m_recv.at[d]).start()

    @pl.loop(1, heads)
    def _(k):
        p = head_at(k, 1)
        to_head(tok_ref.at[p], tbuf.at[d, h], t_send, t_recv, p).start()
        to_head(pair_ref.at[:, cols(p, 2 * HD)], pbuf.at[h], p_send, p_recv, p).start()

    @pl.loop(1, heads)
    def _(k):
        p = head_at(k, 1)
        to_head(q_ref.at[:, cols(p, width)], qbuf.at[h], q_send, q_recv, p).start()

    @pl.loop(1, groups)
    def _(k):
        g = (d + k) % groups
        to_group(leave_ref, mig_out.at[d], m_send, m_recv, g).start()

    @pl.loop(0, heads)
    def _(p):
        landed(tbuf.at[d, p], t_recv.at[p])

    @pl.loop(1, groups)
    def _(k):
        g = (d + k) % groups
        to_group(tbuf.at[d], tbuf.at[d], a_send, a_recv, g).start()

    @pl.loop(0, heads)
    def _(p):
        landed(pbuf.at[p], p_recv.at[p])

    new = pbuf[...].reshape(spare, 2 * HD)
    pair_out[...] = new
    keys[spare:, :] = new[:, :HD]
    values[spare:, :HD] = new[:, HD:]
    values[spare:, HD:] = jnp.ones((spare, HD), jnp.bfloat16)
    old = old_ref[...].astype(jnp.float32)
    seen = lax.broadcasted_iota(jnp.int32, (spare, HD), 0) < prefix[0]
    first = new[0:16, :HD].astype(jnp.float32)[0:1, :]
    keys[:spare, :] = jnp.where(seen, old[:, :HD], first).astype(jnp.bfloat16)
    values[:spare, :HD] = jnp.where(seen, old[:, HD:], 0.0).astype(jnp.bfloat16)
    values[:spare, HD:] = jnp.where(seen, 1.0, 0.0).astype(jnp.bfloat16)

    @pl.loop(0, heads)
    def _(step):
        src = head_at(step, -1)
        landed(qbuf.at[src], q_recv.at[src])
        for case in range(spare // 256):

            @pl.when(src // 2 == case)
            def _(case=case):
                used = spare + 256 * (case + 1)
                row0 = (src % 2) * block

                @pl.loop(0, QPK // 2, unroll=2)
                def _(pair):
                    c0 = pl.multiple_of(pair * 2 * HD, 2 * HD)
                    c1 = pl.multiple_of(pair * 2 * HD + HD, HD)
                    q = jnp.concatenate(
                        [qbuf[src, :, pl.ds(c0, HD)], qbuf[src, :, pl.ds(c1, HD)]], axis=0
                    )
                    out = attend_tile(q, keys[:used, :], values[:used, :], row0, block)
                    out = out.astype(jnp.bfloat16)
                    obuf[src, :, pl.ds(c0, HD)] = out[:block]
                    obuf[src, :, pl.ds(c1, HD)] = out[block:]

        @pl.when(step == 0)
        def _():
            pltpu.make_async_copy(obuf.at[h], out_ref.at[:, cols(h, width)], o_recv.at[h]).start()

        @pl.when(step > 0)
        def _():
            to_head(obuf.at[src], out_ref.at[:, cols(h, width)], o_send, o_recv, src).start()

    @pl.loop(1, groups)
    def _(k):
        g = (d + k) % groups
        landed(tbuf.at[g], a_recv.at[g])
        landed(tbuf.at[d], a_send.at[g])
        landed(mig_out.at[g], m_recv.at[g])
        landed(leave_ref, m_send.at[g])

    landed(mig_out.at[d], m_recv.at[d])
    tok_out[...] = tbuf[...]

    @pl.loop(1, heads)
    def _(k):
        p = (h + k) % heads
        landed(tok_ref.at[p], t_send.at[p])
        landed(pbuf.at[p], p_send.at[p])
        landed(qbuf.at[p], q_send.at[p])
        landed(obuf.at[p], o_send.at[p])

    @pl.loop(0, heads)
    def _(p):
        landed(out_ref.at[:, cols(p, width)], o_recv.at[p])


def prefill(prefix, query, pairs, tokens, leaving, old, heads, groups):
    block, columns = query.shape
    width = columns // heads
    rows = block * heads
    bf16 = jnp.bfloat16
    vmem = pl.BlockSpec(memory_space=pltpu.VMEM)
    hbm = pl.BlockSpec(memory_space=pl.ANY)
    sem = pltpu.SemaphoreType.DMA
    return pl.pallas_call(
        prefill_kernel,
        out_shape=(
            jax.ShapeDtypeStruct((block, columns), bf16),
            jax.ShapeDtypeStruct((rows, 2 * HD), bf16),
            jax.ShapeDtypeStruct((groups,) + tokens.shape, bf16),
            jax.ShapeDtypeStruct((groups,) + leaving.shape, bf16),
        ),
        in_specs=[pl.BlockSpec(memory_space=pltpu.SMEM), hbm, hbm, vmem, vmem, vmem],
        out_specs=(hbm, vmem, vmem, hbm),
        scratch_shapes=[
            pltpu.VMEM((heads, block, width), bf16),
            pltpu.VMEM((heads, block, 2 * HD), bf16),
            pltpu.VMEM((groups,) + tokens.shape, bf16),
            pltpu.VMEM((heads, block, width), bf16),
            pltpu.VMEM((2 * rows, HD), bf16),
            pltpu.VMEM((2 * rows, 2 * HD), bf16),
        ]
        + [sem((heads,))] * 8
        + [sem((groups,))] * 4,
        compiler_params=pltpu.CompilerParams(
            collective_id=0, has_side_effects=True, vmem_limit_bytes=44 * 1024 * 1024
        ),
        name="prefill_exchange",
    )(prefix, query, pairs, tokens, leaving, old)


def gather_kernel(where, dtable, ptable, migrant, pool_ref, leave_ref, old_ref, sem):
    slot = migrant[where[0], 0]
    for j in range(leave_ref.shape[0]):
        pltpu.make_async_copy(pool_ref.at[dtable[slot, j], 0], leave_ref.at[j], sem.at[0]).start()
    for j in range(old_ref.shape[0]):
        pltpu.make_async_copy(pool_ref.at[ptable[0, j], 0], old_ref.at[j], sem.at[1]).start()
    for k, ref in enumerate((leave_ref, old_ref)):
        pltpu.make_async_copy(pool_ref.at[pl.ds(0, ref.shape[0]), 0], ref, sem.at[k]).wait()


def gather(where, dtable, ptable, migrant, pool, prefix_pages):
    vmem = pl.BlockSpec(memory_space=pltpu.VMEM)
    smem = pl.BlockSpec(memory_space=pltpu.SMEM)
    return pl.pallas_call(
        gather_kernel,
        out_shape=tuple(
            jax.ShapeDtypeStruct((n, PAGE, 2 * HD), pool.dtype) for n in (MIGP, prefix_pages)
        ),
        in_specs=[smem] * 4 + [pl.BlockSpec(memory_space=pl.ANY)],
        out_specs=(vmem, vmem),
        scratch_shapes=[pltpu.SemaphoreType.DMA((2,))],
        name="gather_pages",
    )(where, dtable, ptable, migrant, pool)


def decode_kernel(
    where, dtable, ptable, cached, migrant, target, prefix, arrivals,
    tok_ref, mig_ref, new_ref, pool_ref, o_ref, out_ref,
    buf, rows, in_sem, out_sem,
):
    slots = o_ref.shape[0]
    per_slot = buf.shape[1]
    group = where[0]
    my_slot = migrant[group, 0]
    source = lax.fori_loop(
        0, target.shape[0], lambda i, found: jnp.where(target[i, 0] == group, i, found), 0
    )
    incoming = cached[source * slots + migrant[source, 0]]

    @pl.loop(0, slots * per_slot)
    def _(n):
        s, j = n // per_slot, n % per_slot
        moved = jnp.logical_and(s == my_slot, j < MIGP)

        @pl.when(moved)
        def _():
            pltpu.make_async_copy(
                mig_ref.at[source, jnp.minimum(j, MIGP - 1)], buf.at[s, j], in_sem.at[s]
            ).start()

        @pl.when(jnp.logical_not(moved))
        def _():
            pltpu.make_async_copy(pool_ref.at[dtable[s, j], 0], buf.at[s, j], in_sem.at[s]).start()

    for part in range(2):

        @pl.loop(0, per_slot)
        def _(j, part=part):
            page = ptable[0, part * per_slot + j]
            pltpu.make_async_copy(
                pool_ref.at[page, 0], buf.at[slots + part, j], in_sem.at[slots + part]
            ).start()

    @pl.loop(0, arrivals.shape[0])
    def _(i):
        slot = arrivals[i]

        @pl.when(slot // slots == group)
        def _():
            rows[slot % slots] = i

    for s in range(slots):
        pltpu.make_async_copy(pool_ref.at[pl.ds(0, per_slot), 0], buf.at[s], in_sem.at[s]).wait()

        token = tok_ref[rows[s]]
        wide = token.astype(jnp.float32)
        pair = jnp.concatenate([wide[QPK : QPK + 1], wide[QPK + 1 : QPK + 2]], axis=1)
        length = jnp.where(my_slot == s, incoming, cached[group * slots + s])
        page, row = length // PAGE, length % PAGE
        base = pl.multiple_of((row // 16) * 16, 16)
        tile = buf[s, page, pl.ds(base, 16), :].astype(jnp.float32)
        hit = lax.broadcasted_iota(jnp.int32, tile.shape, 0) == row - base
        tile = jnp.where(hit, pair, tile)
        buf[s, page, pl.ds(base, 16), :] = tile.astype(jnp.bfloat16)

        @pl.loop(0, per_slot)
        def _(j, s=s):
            pltpu.make_async_copy(buf.at[s, j], out_ref.at[dtable[s, j], 0], out_sem.at[s]).start()

        kv = buf[s].reshape(per_slot * PAGE, 2 * HD)
        scores = lax.dot_general(token, kv[:, :HD], NT, preferred_element_type=jnp.float32)
        seen = lax.broadcasted_iota(jnp.int32, scores.shape, 1) <= length
        scores = jnp.where(seen, scores, NEG)
        top = jnp.max(scores, axis=1, keepdims=True)
        weights = jnp.exp2((scores - top) * (HD**-0.5 * LOG2E))
        total = jnp.sum(weights, axis=1, keepdims=True)
        mixed = jnp.dot(weights.astype(jnp.bfloat16), kv[:, HD:], preferred_element_type=jnp.float32)
        o_ref[s] = (mixed / total)[:QPK].astype(jnp.bfloat16)

    first = prefix[0] // PAGE
    for part in range(2):
        at = slots + part
        pltpu.make_async_copy(pool_ref.at[pl.ds(0, per_slot), 0], buf.at[at], in_sem.at[at]).wait()

        @pl.loop(0, per_slot)
        def _(j, part=part, at=at):
            logical = part * per_slot + j
            page = ptable[0, logical]
            fresh = jnp.logical_and(logical >= first, logical < first + 16)

            @pl.when(fresh)
            def _():
                pltpu.make_async_copy(
                    new_ref.at[logical - first], out_ref.at[page, 0], out_sem.at[at]
                ).start()

            @pl.when(jnp.logical_not(fresh))
            def _():
                pltpu.make_async_copy(buf.at[at, j], out_ref.at[page, 0], out_sem.at[at]).start()

    for at in range(slots + 2):
        pltpu.make_async_copy(buf.at[at], out_ref.at[pl.ds(0, per_slot), 0], out_sem.at[at]).wait()


def decode_and_store(
    where, dtable, ptable, cached, migrant, target, prefix, arrivals, tokens, moved, pair_all, pool
):
    slots, per_slot = dtable.shape
    vmem = pl.BlockSpec(memory_space=pltpu.VMEM)
    smem = pl.BlockSpec(memory_space=pltpu.SMEM)
    hbm = pl.BlockSpec(memory_space=pl.ANY)
    return pl.pallas_call(
        decode_kernel,
        out_shape=(
            jax.ShapeDtypeStruct((slots, QPK, HD), jnp.bfloat16),
            jax.ShapeDtypeStruct(pool.shape, pool.dtype),
        ),
        in_specs=[smem] * 8 + [vmem, hbm, vmem, hbm],
        out_specs=(vmem, hbm),
        scratch_shapes=[
            pltpu.VMEM((slots + 2, per_slot, PAGE, 2 * HD), jnp.bfloat16),
            pltpu.SMEM((slots,), jnp.int32),
            pltpu.SemaphoreType.DMA((slots + 2,)),
            pltpu.SemaphoreType.DMA((slots + 2,)),
        ],
        compiler_params=pltpu.CompilerParams(vmem_limit_bytes=24 * 1024 * 1024),
        cost_estimate=pl.CostEstimate(
            flops=2 * 64 * 1024 * 256, bytes_accessed=11 << 20, transcendentals=64 * 1024
        ),
        name="decode_and_pool",
    )(
        where, dtable, ptable, cached, migrant, target, prefix, arrivals, tokens, moved, pair_all,
        pool,
    )


def per_device(
    prefill_query,
    prefill_pairs,
    decode_query,
    decode_pairs,
    cache_pool,
    decode_pages,
    prefill_pages,
    cache_length,
    prefix_length,
    migrant_slot,
    migrant_target,
    arrivals,
):
    where = lax.axis_index("dp").astype(jnp.int32).reshape(1)
    heads = lax.axis_size("head")
    groups = lax.axis_size("dp")
    slot_count = decode_pages.shape[0]
    prefix_pages = prefill_pages.shape[1] // 2

    leaving, old = gather(
        where, decode_pages, prefill_pages, migrant_slot, cache_pool, prefix_pages
    )
    leaving = leaving.reshape(-1, 2 * HD)
    old = old.reshape(-1, 2 * HD)
    tokens = jnp.concatenate(
        [
            decode_query.reshape(heads, QPK, HD),
            decode_pairs.reshape(heads, 2, HD),
            jnp.zeros((heads, 6, HD), jnp.bfloat16),
        ],
        axis=1,
    )
    prefill_attended, pair_all, all_tokens, all_leaving = prefill(
        prefix_length, prefill_query, prefill_pairs, tokens, leaving, old, heads, groups
    )

    decoded, new_pool = decode_and_store(
        where, decode_pages, prefill_pages, cache_length, migrant_slot, migrant_target,
        prefix_length, arrivals, all_tokens.reshape(groups * slot_count, -1, HD),
        all_leaving.reshape(groups, MIGP, PAGE, 2 * HD), pair_all.reshape(-1, PAGE, 2 * HD),
        cache_pool,
    )
    return (prefill_attended, decoded.reshape(slot_count, -1), new_pool)


def solution(mesh):
    placed = (
        P(("dp", "head"), None),
        P(("dp", "head"), None),
        P(("dp", "head"), None),
        P(("dp", "head"), None),
        P("dp", "head", None, None),
        P("dp", None),
        P("dp", None),
        P(),
        P("dp"),
        P(),
        P(),
        P(),
    )
    return jax.shard_map(
        per_device,
        mesh=mesh,
        in_specs=placed,
        out_specs=(P(("dp", "head"), None), P("dp", "head"), P("dp", "head", None, None)),
        check_vma=False,
    )
```
